256 devices in a mesh: ep: 64 (over y_lo, z, x), fsdp: 4 (over y_hi, core).
Axes of the slice: x: 4, y: 4 (y_hi: 2, y_lo: 2; y = y_hi * 2 + y_lo), z: 8, core: 2. Of those that a mesh axis runs over, the one named last changes fastest.
Arguments:
- tokens: bfloat16 [12288, 4096], P(('ep', 'fsdp')), may hold values from -6 to 6
- expert_ids: int32 [12288, 8], P(('ep', 'fsdp')), may hold values from 0 to 63, all different within a row; in each aligned block of 48 rows (0 to 47, 48 to 95, ...) at most 9 rows name the same one
- gate_values: float32 [12288, 8], P(('ep', 'fsdp')), may hold values from 0.05 to 1
- gate_weight: bfloat16 [64, 4096, 1024], P('ep', None, 'fsdp'), may hold values from -0.09375 to 0.09375
- up_weight: bfloat16 [64, 4096, 1024], P('ep', None, 'fsdp'), may hold values from -0.09375 to 0.09375
- down_weight: bfloat16 [64, 4096, 1024], P('ep', None, 'fsdp'), may hold values from -0.1875 to 0.1875
Outputs:
- mixed: bfloat16 [12288, 4096], P(('ep', 'fsdp'))
The draws below stay inside these ranges and needn't reach their ends.
Inputs may be any that keep to these rules, and one draw needn't show every extreme that they name: `expert_ids`: each row names 8 different experts. Among the rows of one device's aligned block of 48 tokens no expert is named more than 9 times, and in some blocks one expert is named exactly 9 times.
All inputs are finite; a program needn't handle non-finite values.
Results may differ from the reference program's by a relative error of at most 0.0057.
Values may be sent and summed in bfloat16 or wider, within the bound.
No kernel may reach another device: no remote copies, remote signals or barrier semaphores. Data moves between devices by JAX's collectives and lax.ppermute only.
A program may use at most 128 MiB of HBM per device.

```python
import math
import jax
import jax.numpy as jnp
import numpy as np
from jax import lax

D = 4096
FWIN = 1024
TOPK = 8
TOK_DEV = 48
EXPERTS = 64
CAP = 9
TOKENS = 12288


def levels(stream_key, shape, cuts, smallest, largest):
    factor_of, own = 1.0, jax.random.fold_in(stream_key, 6)
    for position, shards_of in cuts:
        draws = jnp.exp(jax.random.uniform(jax.random.fold_in(own, position), (shards_of,), jnp.float32, smallest / len(cuts), largest / len(cuts)))
        factor_of = factor_of * jnp.repeat(draws, shape[position] // shards_of).reshape([-1 if axis == position else 1 for axis in range(len(shape))])
    return factor_of


def deal_out(key, own, number, rows, count, top, limit, lean):
    ranking = jax.random.permutation(key, count)
    crowded, usual = shares(count, rows * top, limit, lean, True), shares(count, rows * top, limit, lean, False)
    places = jnp.arange(count)

    def named(tallies, offset_by):
        used = int((tallies > 0).sum())
        fixed = max(1, used // 4)
        moved = fixed + (places - fixed + offset_by * (used - fixed)) % max(1, count - fixed)
        return jnp.zeros((count,), jnp.int32).at[ranking[jnp.where(places < fixed, places, moved)]].set(jnp.asarray(tallies, jnp.int32))

    tallies = jnp.where(number % 4 == 0, named(crowded, number // 4), named(usual, number - number // 4 - 1))
    mixed = jax.random.permutation(jax.random.fold_in(own, 3), count)
    donor, receiver = mixed[0:count // 2 * 2:2], mixed[1:count // 2 * 2:2]
    slack = jnp.minimum(tallies[donor] - 1, limit - tallies[receiver]) // 2
    slack = jnp.where((donor == ranking[0]) | (receiver == ranking[0]) | (tallies[receiver] == 0), 0, jnp.maximum(slack, 0))
    moved = jax.random.randint(jax.random.fold_in(own, 4), (count // 2,), 0, 1 << 20) % (slack + 1)
    tallies = tallies.at[donor].add(-moved).at[receiver].add(moved)
    members = jnp.searchsorted(jnp.cumsum(tallies), jnp.arange(rows * top), side="right").astype(jnp.int32)
    table = members.reshape(top, rows).T
    table = table[jax.random.permutation(jax.random.fold_in(own, 1), rows)]
    offset_by = jax.random.randint(jax.random.fold_in(own, 2), (rows, 1), 0, top)
    return jnp.take_along_axis(table, (jnp.arange(top)[None, :] + offset_by) % top, axis=1)


def shares(amount, total, reach, skew, full):
    portions = [(1 << 20) // math.isqrt(grade ** skew) + 1 for grade in range(1, amount + 1)]
    largest = reach if full else min(reach, max(-(-total // amount), total * portions[0] // sum(portions)))
    least = 1 if total - largest >= amount - 1 else 0
    given, spare = [largest] + [least] * (amount - 1), total - largest - least * (amount - 1)
    while spare > 0:
        movable = [i for i in range(1, amount) if given[i] < largest] or [i for i in range(1, amount) if given[i] < reach]
        mass, remaining = sum([portions[i] for i in movable]), spare
        for i in movable:
            more = min(reach - given[i], max(1, remaining * portions[i] // mass), spare)
            given[i] = given[i] + more
            spare = spare - more
    return np.array(given)


def noise(rng, extent, scale, reach, cuts=(), kind=jnp.bfloat16):
    gain = levels(rng, extent, cuts, -0.22, 0.18) if cuts else 1.0
    values = jax.random.normal(rng, extent, jnp.float32) * scale * gain
    return jnp.minimum(jnp.maximum(values, -reach), reach).astype(kind)


def setup_inputs(seed: int = 0) -> dict:
    keys = jax.random.split(jax.random.key(seed), 7)
    tokens = noise(keys[0], (TOKENS, D), 1.0, 6.0, ((0, 256),))
    expert_ids_keys = jax.random.split(jax.random.fold_in(keys[1], 1), TOKENS // TOK_DEV)
    expert_ids_turns = jax.random.permutation(jax.random.fold_in(keys[1], 3), TOKENS // TOK_DEV)
    expert_ids = jax.vmap(lambda own, number: deal_out(jax.random.fold_in(keys[1], 2), own, number, TOK_DEV, EXPERTS, TOPK, CAP, 2))(expert_ids_keys, expert_ids_turns).reshape((TOKENS, TOPK))
    gate_values = jnp.clip(jnp.exp(math.log(1.0) - 2.9957323 * jax.random.uniform(keys[2], (TOKENS, TOPK), jnp.float32) ** levels(keys[2], (TOKENS, TOPK), ((0, 256),), -0.2, 0.2)), 0.05, 1.0)
    gate_weight = noise(keys[3], (EXPERTS, D, FWIN), D ** -0.5, 0.09375, ((0, 64), (2, 4)))
    up_weight = noise(keys[4], (EXPERTS, D, FWIN), D ** -0.5, 0.09375, ((0, 64), (2, 4)))
    down_weight = noise(keys[5], (EXPERTS, D, FWIN), FWIN ** -0.5, 0.1875, ((0, 64), (2, 4)))
    return dict(tokens=tokens, expert_ids=expert_ids, gate_values=gate_values, gate_weight=gate_weight, up_weight=up_weight, down_weight=down_weight)


def expert_apply(gathered, gate_matrix, up_matrix, down_matrix):
    gate_part = jnp.dot(gathered, gate_matrix, preferred_element_type=jnp.float32)
    up_part = jnp.dot(gathered, up_matrix, preferred_element_type=jnp.float32)
    hidden = (jax.nn.silu(gate_part) * up_part).astype(jnp.bfloat16)
    result = lax.dot_general(hidden, down_matrix, (((1,), (1,)), ((), ())), preferred_element_type=jnp.float32)
    return result.astype(jnp.bfloat16)


def reference(tokens, expert_ids, gate_values, gate_weight, up_weight, down_weight):
    blocks = TOKENS // TOK_DEV
    pair_count = TOK_DEV * TOPK
    block_ids = expert_ids.reshape(blocks, pair_count)
    onehot = (block_ids[:, :, None] == jnp.arange(EXPERTS, dtype=jnp.int32)[None, None, :]).astype(jnp.int32)
    earlier = jnp.cumsum(onehot, axis=1) - onehot
    slot_index = jnp.sum(earlier * onehot, axis=2).astype(jnp.int32)
    token_of = (jnp.arange(blocks, dtype=jnp.int32)[:, None] * TOK_DEV
                + jnp.arange(pair_count, dtype=jnp.int32)[None, :] // TOPK).astype(jnp.int32)
    block_of = jnp.broadcast_to(jnp.arange(blocks, dtype=jnp.int32)[:, None], (blocks, pair_count))
    token_table = jnp.full((EXPERTS, blocks, CAP), TOKENS, dtype=jnp.int32)
    token_table = token_table.at[block_ids, block_of, slot_index].set(token_of)
    gate_table = jnp.zeros((EXPERTS, blocks, CAP), dtype=jnp.float32)
    gate_table = gate_table.at[block_ids, block_of, slot_index].set(gate_values.reshape(blocks, pair_count))
    padded = jnp.concatenate([tokens, jnp.zeros((1, D), dtype=jnp.bfloat16)], axis=0)

    def expert_step(summed, expert):
        targets = token_table[expert].reshape(-1)
        gathered = padded[targets]
        result = expert_apply(gathered, gate_weight[expert], up_weight[expert], down_weight[expert])
        weights_here = gate_table[expert].reshape(-1)
        summed = summed.at[targets].add(weights_here[:, None] * result.astype(jnp.float32), mode="drop")
        return summed, None

    summed, unused = lax.scan(expert_step, jnp.zeros((TOKENS, D), dtype=jnp.float32), jnp.arange(EXPERTS, dtype=jnp.int32))
    return summed.astype(jnp.bfloat16)
```

```python
import jax
import jax.numpy as jnp
from jax import lax
from jax.sharding import Mesh, PartitionSpec as P

NYL, NZ, NX, NYH, NC = 2, 8, 4, 2, 2
AXES = ("yl", "z", "x", "yh", "core")
IN_CHUNKS = 2
OUT_CHUNKS = 4
CAP = 9


def plane_groups():
    def index(yl, z, x, yh, core):
        return (((yl * NZ + z) * NX + x) * NYH + yh) * NC + core

    groups = []
    for z in range(NZ):
        for core in range(NC):
            for half in range(NYH):
                groups.append(
                    [index(yl, z, x, half ^ (yl if core else 0), core) for yl in range(NYL) for x in range(NX)]
                )
    return groups


def exchange(block):
    return lax.all_to_all(
        block, AXES, 0, 0, axis_index_groups=plane_groups(), tiled=True
    )


def swap(block, axis):
    return lax.ppermute(block, axis, [(0, 1), (1, 0)])


def local(tokens, expert_ids, gate_values, gate_weight, up_weight, down_weight):
    rows, width = tokens.shape
    dests = NYL * NX
    cap = CAP * NZ
    in_width = width // IN_CHUNKS
    out_width = width // OUT_CHUNKS

    own_gate, own_up, own_down = gate_weight[0], up_weight[0], down_weight[0]

    def pieces(own):
        far = swap(own, "yh")
        return [own, swap(own, "core"), far, swap(far, "core")]

    gates = pieces(own_gate)
    ups = pieces(own_up)
    downs = [
        pieces(own_down[c * out_width : (c + 1) * out_width]) for c in range(OUT_CHUNKS)
    ]

    meta = jnp.concatenate([expert_ids.astype(jnp.float32), gate_values], axis=1)
    meta = lax.all_gather(meta, "z", axis=0, tiled=True)
    parts = [
        lax.all_gather(tokens[:, c * in_width : (c + 1) * in_width], "z", axis=0, tiled=True)
        for c in range(IN_CHUNKS)
    ]

    count = NZ * rows
    top = expert_ids.shape[1]
    ids = meta[:, :top].astype(jnp.int32)
    values = meta[:, top:]
    dest = jnp.arange(dests, dtype=jnp.int32)
    expert = (dest // NX) * (NZ * NX) + lax.axis_index("z") * NX + dest % NX
    hit = ids[:, :, None] == expert[None, None, :]
    named = jnp.any(hit, axis=1)
    weight = jnp.sum(jnp.where(hit, values[:, :, None], 0.0), axis=1)
    order = jnp.arange(count, dtype=jnp.int32)
    before = (order[None, :] < order[:, None]).astype(jnp.bfloat16)
    rank = jnp.dot(before, named.astype(jnp.bfloat16), preferred_element_type=jnp.float32).astype(jnp.int32)
    slot = jnp.where(named, rank + cap * dest[None, :], -1)
    slots = jnp.arange(dests * cap, dtype=jnp.int32)
    owner = slots // cap
    slot_of = jnp.repeat(slot, cap, axis=1)
    weight_of = jnp.repeat(weight, cap, axis=1)
    here = slot_of == slots[None, :]
    pack = here.astype(jnp.bfloat16)
    scale = jnp.where(here, weight_of, 0.0)
    scale_hi = scale.astype(jnp.bfloat16)
    scale_lo = (scale - scale_hi.astype(jnp.float32)).astype(jnp.bfloat16)

    arrived = []
    for part in parts:
        packed = lax.dot_general(pack, part, (((0,), (0,)), ((), ())), preferred_element_type=jnp.float32)
        packed = packed.astype(jnp.bfloat16).reshape(dests, cap, in_width)
        arrived.append(exchange(packed).reshape(dests * cap, in_width))

    def project(weights):
        whole = jnp.concatenate(weights, axis=1)
        total = None
        for c, block in enumerate(arrived):
            term = jnp.dot(block, whole[c * in_width : (c + 1) * in_width], preferred_element_type=jnp.float32)
            total = term if total is None else total + term
        return total

    gate_part = project(gates)
    up_part = project(ups)
    hidden = (jax.nn.silu(gate_part) * up_part).astype(jnp.bfloat16)

    mixed = []
    for c in range(OUT_CHUNKS):
        whole = jnp.concatenate(downs[c], axis=1)
        out = lax.dot_general(hidden, whole, (((1,), (1,)), ((), ())), preferred_element_type=jnp.float32)
        out = exchange(out.astype(jnp.bfloat16).reshape(dests, cap, out_width)).reshape(dests * cap, out_width)
        both = jnp.dot(scale_hi, out, preferred_element_type=jnp.float32) + jnp.dot(
            scale_lo, out, preferred_element_type=jnp.float32
        )
        mixed.append(lax.psum_scatter(both.astype(jnp.bfloat16), "z", scatter_dimension=0, tiled=True))
    return jnp.concatenate(mixed, axis=1)


def solution(mesh):
    fine = Mesh(mesh.devices.reshape(NYL, NZ, NX, NYH, NC), AXES)
    rows = P(AXES, None)
    weights = P(("yl", "z", "x"), None, ("yh", "core"))
    return jax.shard_map(
        local,
        mesh=fine,
        in_specs=(rows, rows, rows, weights, weights, weights),
        out_specs=rows,
        check_vma=False,
    )
```

```python
import jax
import jax.numpy as jnp
from jax import lax
from jax.sharding import Mesh, PartitionSpec as P

NYL, NZ, NX, NYH, NC = 2, 8, 4, 2, 2
AXES = ("yl", "z", "x", "yh", "core")
IN_CHUNKS = 1
OUT_CHUNKS = 2
CAP = 9


def plane_groups():
    def index(yl, z, x, yh, core):
        return (((yl * NZ + z) * NX + x) * NYH + yh) * NC + core

    groups = []
    for z in range(NZ):
        for core in range(NC):
            for half in range(NYH):
                groups.append(
                    [index(yl, z, x, half ^ (yl if core else 0), core) for yl in range(NYL) for x in range(NX)]
                )
    return groups


def exchange(block):
    return lax.all_to_all(
        block, AXES, 0, 0, axis_index_groups=plane_groups(), tiled=True
    )


def swap(block, axis):
    return lax.ppermute(block, axis, [(0, 1), (1, 0)])


def spread(block):
    copies = jnp.broadcast_to(block[None], (NZ,) + block.shape)
    full = lax.all_to_all(copies, "z", 0, 0, tiled=True)
    return full.reshape(NZ * block.shape[0], block.shape[1])


def local(tokens, expert_ids, gate_values, gate_weight, up_weight, down_weight):
    rows, width = tokens.shape
    dests = NYL * NX
    cap = CAP * NZ
    in_width = width // IN_CHUNKS
    out_width = width // OUT_CHUNKS

    own_gate, own_up, own_down = gate_weight[0], up_weight[0], down_weight[0]

    def pieces(own):
        far = swap(own, "yh")
        near = swap(own, "core")
        hop = swap(far, "core")
        return [own, near, far, hop]

    gates = pieces(own_gate)
    ups = pieces(own_up)
    downs = [pieces(own_down[c * out_width : (c + 1) * out_width]) for c in range(OUT_CHUNKS)]

    meta = jnp.concatenate([expert_ids.astype(jnp.float32), gate_values], axis=1)
    meta = spread(meta)
    parts = []
    for c in range(IN_CHUNKS):
        parts.append(spread(tokens[:, c * in_width : (c + 1) * in_width]))

    count = NZ * rows
    top = expert_ids.shape[1]
    ids = meta[:, :top].astype(jnp.int32)
    values = meta[:, top:]
    dest = jnp.arange(dests, dtype=jnp.int32)
    expert = (dest // NX) * (NZ * NX) + lax.axis_index("z") * NX + dest % NX
    hit = ids[:, :, None] == expert[None, None, :]
    named = jnp.any(hit, axis=1)
    weight = jnp.sum(jnp.where(hit, values[:, :, None], 0.0), axis=1)
    order = jnp.arange(count, dtype=jnp.int32)
    before = (order[None, :] < order[:, None]).astype(jnp.bfloat16)
    rank = jnp.dot(before, named.astype(jnp.bfloat16), preferred_element_type=jnp.float32).astype(jnp.int32)
    slot = jnp.where(named, rank + cap * dest[None, :], -1)
    slots = jnp.arange(dests * cap, dtype=jnp.int32)
    pack = (jnp.repeat(slot, cap, axis=1) == slots[None, :]).astype(jnp.bfloat16)

    def turned(table):
        return lax.dynamic_slice_in_dim(jnp.concatenate([table, table]), lax.axis_index("z") * rows, count)

    here = jnp.repeat(turned(slot), cap, axis=1) == slots[None, :]
    scale = jnp.where(here, jnp.repeat(turned(weight), cap, axis=1), 0.0)
    scale_hi = scale.astype(jnp.bfloat16)
    scale_lo = (scale - scale_hi.astype(jnp.float32)).astype(jnp.bfloat16)

    arrived = []
    for part in parts:
        packed = lax.dot_general(pack, part, (((0,), (0,)), ((), ())), preferred_element_type=jnp.float32)
        packed = packed.astype(jnp.bfloat16).reshape(dests, cap, in_width)
        arrived.append(exchange(packed).reshape(dests * cap, in_width))

    def project(weights):
        whole = jnp.concatenate(weights, axis=1)
        total = None
        for c, block in enumerate(arrived):
            term = jnp.dot(block, whole[c * in_width : (c + 1) * in_width], preferred_element_type=jnp.float32)
            total = term if total is None else total + term
        return total

    gate_part = project(gates)
    up_part = project(ups)
    hidden = (jax.nn.silu(gate_part) * up_part).astype(jnp.bfloat16)

    mixed = []
    for c in range(OUT_CHUNKS):
        whole = jnp.concatenate(downs[c], axis=1)
        out = lax.dot_general(hidden, whole, (((1,), (1,)), ((), ())), preferred_element_type=jnp.float32)
        out = out.astype(jnp.bfloat16).reshape(dests, cap, out_width)
        out = exchange(out).reshape(dests * cap, out_width)
        both = jnp.dot(scale_hi, out, preferred_element_type=jnp.float32) + jnp.dot(
            scale_lo, out, preferred_element_type=jnp.float32
        )
        both = both.astype(jnp.bfloat16).reshape(NZ, rows, out_width)
        total = both[0].astype(jnp.float32)
        for step in (4, 3, 5, 2, 6, 1, 7):
            term = lax.ppermute(both[step], "z", [(i, (i + step) % NZ) for i in range(NZ)])
            total = total + term.astype(jnp.float32)
        mixed.append(total.astype(jnp.bfloat16))
    return jnp.concatenate(mixed, axis=1)


def solution(mesh):
    fine = Mesh(mesh.devices.reshape(NYL, NZ, NX, NYH, NC), AXES)
    rows = P(AXES, None)
    weights = P(("yl", "z", "x"), None, ("yh", "core"))
    return jax.shard_map(
        local,
        mesh=fine,
        in_specs=(rows, rows, rows, weights, weights, weights),
        out_specs=rows,
        check_vma=False,
    )
```

```python
import jax
import jax.numpy as jnp
from jax import lax
from jax.experimental.layout import Layout, with_layout_constraint
from jax.sharding import Mesh, PartitionSpec as P

NYL, NZ, NX, NYH, NC = 2, 8, 4, 2, 2
AXES = ("yl", "z", "x", "yh", "core")
STEPS = (4, 3, 7, 2, 6, 1, 5)
CAP = 9
EXTRA = 128
UP = (1024, 3072)
OUT = (1792, 2304)


def plane_groups():
    def index(yl, z, x, yh, core):
        return (((yl * NZ + z) * NX + x) * NYH + yh) * NC + core

    groups = []
    for z in range(NZ):
        for core in range(NC):
            for half in range(NYH):
                groups.append(
                    [index(yl, z, x, half ^ (yl if core else 0), core) for yl in range(NYL) for x in range(NX)]
                )
    return groups


def exchange(block):
    return lax.all_to_all(
        block, AXES, 0, 0, axis_index_groups=plane_groups(), tiled=True
    )


def swap(block, axis):
    return lax.ppermute(block, axis, [(0, 1), (1, 0)])


def along_z(block, step):
    return lax.ppermute(block, "z", [(i, (i + step) % NZ) for i in range(NZ)])


def gathered(own, sizes):
    near = swap(own, "core")
    blocks, start = [], 0
    for size in sizes:
        part = slice(start, start + size)
        far = swap(own[part], "yh")
        hop = swap(far, "core")
        blocks.append(jnp.concatenate([own[part], near[part], far, hop], axis=1))
        start += size
    return blocks


def three_parts(value):
    parts = []
    for _ in range(3):
        part = value.astype(jnp.bfloat16)
        value = value - part.astype(jnp.float32)
        parts.append(part)
    return parts


def local(tokens, expert_ids, gate_values, gate_weight, up_weight, down_weight):
    rows, width = tokens.shape
    top = expert_ids.shape[1]
    dests = NYL * NX
    cap = CAP * NZ

    gate = gathered(gate_weight[0], (width,))[0]
    ups = gathered(up_weight[0], UP)
    downs = gathered(down_weight[0], OUT)

    notes = jnp.concatenate([expert_ids.astype(jnp.bfloat16)] + three_parts(gate_values), axis=1)
    notes = jnp.pad(notes, ((0, 0), (0, EXTRA - notes.shape[1])))
    own = jnp.concatenate([notes, tokens], axis=1)
    blocks = [own]
    for way in (1, -1):
        block = own
        for _ in range(1, NZ // 2 + (way > 0)):
            block = along_z(block, way)
            blocks.append(block)
    whole = jnp.concatenate(blocks, axis=0)
    whole = with_layout_constraint(whole, Layout(major_to_minor=(0, 1)))

    count = NZ * rows
    notes = whole[:, : 4 * top].astype(jnp.float32)
    ids = notes[:, :top].astype(jnp.int32)
    values = notes[:, top : 2 * top] + notes[:, 2 * top : 3 * top] + notes[:, 3 * top :]
    dest = jnp.arange(dests, dtype=jnp.int32)
    expert = (dest // NX) * (NZ * NX) + lax.axis_index("z") * NX + dest % NX
    hit = ids[:, :, None] == expert[None, None, :]
    named = jnp.any(hit, axis=1)
    weight = jnp.sum(jnp.where(hit, values[:, :, None], 0.0), axis=1)
    order = jnp.arange(count, dtype=jnp.int32)
    before = (order[None, :] < order[:, None]).astype(jnp.bfloat16)
    rank = jnp.dot(before, named.astype(jnp.bfloat16), preferred_element_type=jnp.float32).astype(jnp.int32)
    slot = jnp.where(named, rank + cap * dest[None, :], -1)
    slots = jnp.arange(dests * cap, dtype=jnp.int32)
    here = jnp.repeat(slot, cap, axis=1) == slots[None, :]
    pack = here.astype(jnp.bfloat16)
    scale = jnp.where(here, jnp.repeat(weight, cap, axis=1), 0.0)
    scale_hi, scale_lo, _ = three_parts(scale)

    packed = lax.dot_general(pack, whole[:, EXTRA:], (((0,), (0,)), ((), ())), preferred_element_type=jnp.float32)
    packed = packed.astype(jnp.bfloat16).reshape(dests, cap, width)
    arrived = exchange(packed).reshape(dests * cap, width)

    gate_part = jnp.dot(arrived, gate, preferred_element_type=jnp.float32)
    up_part = jnp.dot(arrived[:, : UP[0]], ups[0], preferred_element_type=jnp.float32)
    up_part = jnp.dot(arrived[:, UP[0] :], ups[1], preferred_element_type=jnp.float32) + up_part
    hidden = (jax.nn.silu(gate_part) * up_part).astype(jnp.bfloat16)

    mixed = []
    for c, size in enumerate(OUT):
        out = lax.dot_general(hidden, downs[c], (((1,), (1,)), ((), ())), preferred_element_type=jnp.float32)
        out = out.astype(jnp.bfloat16).reshape(dests, cap, size)
        out = exchange(out).reshape(dests * cap, size)
        both = jnp.dot(scale_hi, out, preferred_element_type=jnp.float32) + jnp.dot(
            scale_lo, out, preferred_element_type=jnp.float32
        )
        both = both.astype(jnp.bfloat16).reshape(NZ, rows, size)
        total = both[0].astype(jnp.float32)
        for place in STEPS:
            term = along_z(both[place], -place if place <= NZ // 2 else place - NZ // 2)
            total = total + term.astype(jnp.float32)
        mixed.append(total.astype(jnp.bfloat16))
    return jnp.concatenate(mixed, axis=1)


def solution(mesh):
    fine = Mesh(mesh.devices.reshape(NYL, NZ, NX, NYH, NC), AXES)
    rows = P(AXES, None)
    weights = P(("yl", "z", "x"), None, ("yh", "core"))
    return jax.shard_map(
        local,
        mesh=fine,
        in_specs=(rows, rows, rows, weights, weights, weights),
        out_specs=rows,
        check_vma=False,
    )
```

```python
import jax
import jax.numpy as jnp
from jax import lax
from jax.experimental.layout import Layout, with_layout_constraint
from jax.sharding import Mesh, PartitionSpec as P

NYL, NZ, NX, NYH, NC = 2, 8, 4, 2, 2
AXES = ("yl", "z", "x", "yh", "core")
STEPS = (4, 3, 7, 2, 6, 1, 5)
CAP = 9
EXTRA = 128
OUT = (1792, 2304)


def plane_groups():
    def index(yl, z, x, yh, core):
        return (((yl * NZ + z) * NX + x) * NYH + yh) * NC + core

    groups = []
    for z in range(NZ):
        for core in range(NC):
            for half in range(NYH):
                groups.append(
                    [index(yl, z, x, half ^ (yl if core else 0), core) for yl in range(NYL) for x in range(NX)]
                )
    return groups


def exchange(block):
    return lax.all_to_all(
        block, AXES, 0, 0, axis_index_groups=plane_groups(), tiled=True
    )


def swap(block, axis):
    return lax.ppermute(block, axis, [(0, 1), (1, 0)])


def along_z(block, step):
    return lax.ppermute(block, "z", [(i, (i + step) % NZ) for i in range(NZ)])


def parts_of(value, count):
    parts = []
    for _ in range(count):
        part = value.astype(jnp.bfloat16)
        value = value - part.astype(jnp.float32)
        parts.append(part)
    return parts


def local(tokens, expert_ids, gate_values, gate_weight, up_weight, down_weight):
    rows, width = tokens.shape
    top = expert_ids.shape[1]
    dests = NYL * NX
    cap = CAP * NZ

    own_gate, own_up, own_down = gate_weight[0], up_weight[0], down_weight[0]
    near_gate, near_up, near_down = swap(own_gate, "core"), swap(own_up, "core"), swap(own_down, "core")
    far_gate = swap(own_gate, "yh")
    far_up = swap(own_up, "yh")
    hop = swap(jnp.concatenate([far_gate, far_up], axis=0), "core")
    gate = jnp.concatenate([own_gate, near_gate, far_gate, hop[:width]], axis=1)
    up = jnp.concatenate([own_up, near_up, far_up, hop[width:]], axis=1)
    downs, start = [], 0
    for size in OUT:
        part = slice(start, start + size)
        far = swap(own_down[part], "yh")
        hop = swap(far, "core")
        downs.append(jnp.concatenate([own_down[part], near_down[part], far, hop], axis=1))
        start += size

    notes = jnp.concatenate([expert_ids.astype(jnp.bfloat16)] + parts_of(gate_values, 2), axis=1)
    notes = jnp.pad(notes, ((0, 0), (0, EXTRA - notes.shape[1])))
    own = jnp.concatenate([notes, tokens], axis=1)
    blocks = [own]
    for way in (1, -1):
        block = own
        for hop in range(1, NZ // 2 + (way > 0)):
            block = along_z(block, way)
            blocks.append(block)
    whole = jnp.concatenate(blocks, axis=0)
    whole = with_layout_constraint(whole, Layout(major_to_minor=(0, 1)))

    count = NZ * rows
    notes = whole[:, : 3 * top].astype(jnp.float32)
    ids = notes[:, :top].astype(jnp.int32)
    values = notes[:, top : 2 * top] + notes[:, 2 * top :]
    dest = jnp.arange(dests, dtype=jnp.int32)
    expert = (dest // NX) * (NZ * NX) + lax.axis_index("z") * NX + dest % NX
    hit = ids[:, :, None] == expert[None, None, :]
    named = jnp.any(hit, axis=1)
    weight = jnp.sum(jnp.where(hit, values[:, :, None], 0.0), axis=1)
    order = jnp.arange(count, dtype=jnp.int32)
    before = (order[None, :] < order[:, None]).astype(jnp.bfloat16)
    rank = jnp.dot(before, named.astype(jnp.bfloat16), preferred_element_type=jnp.float32).astype(jnp.int32)
    slot = jnp.where(named, rank + cap * dest[None, :], -1)
    slots = jnp.arange(dests * cap, dtype=jnp.int32)

    def placed(slot):
        return (jnp.repeat(slot, cap, axis=1) == slots[None, :]).astype(jnp.bfloat16)

    pack = placed(slot)
    back = lax.rem(lax.axis_index("z") - jnp.arange(NZ, dtype=jnp.int32) + NZ, NZ)
    back = jnp.where(back > NZ // 2, NZ + NZ // 2 - back, back)
    unpack = placed(slot.reshape(NZ, rows, dests)[back].reshape(count, dests))

    weights = jnp.pad(jnp.concatenate(parts_of(weight, 2), axis=1), ((0, 0), (0, EXTRA - 2 * dests)))
    whole = lax.dynamic_update_slice(whole, weights, (0, 0))
    packed = lax.dot_general(pack, whole, (((0,), (0,)), ((), ())), preferred_element_type=jnp.float32)
    packed = packed.astype(jnp.bfloat16).reshape(dests, cap, EXTRA + width)
    arrived = exchange(packed).reshape(dests * cap, EXTRA + width)
    mine = lax.axis_index("yl") * NX + lax.axis_index("x")
    weight = arrived[:, : 2 * dests].astype(jnp.float32)
    weight = jnp.where(jnp.arange(2 * dests) % dests == mine, weight, 0.0)
    weight = jnp.sum(weight, axis=1, keepdims=True)
    arrived = arrived[:, EXTRA:]

    gate_part = jnp.dot(arrived, gate, preferred_element_type=jnp.float32)
    up_part = jnp.dot(arrived, up, preferred_element_type=jnp.float32)
    hidden = (jax.nn.silu(gate_part) * up_part).astype(jnp.bfloat16)

    mixed = []
    for c, size in enumerate(OUT):
        out = lax.dot_general(hidden, downs[c], (((1,), (1,)), ((), ())), preferred_element_type=jnp.float32)
        out = (out * weight).astype(jnp.bfloat16).reshape(dests, cap, size)
        out = exchange(out).reshape(dests * cap, size)
        last = c == len(OUT) - 1
        both = jnp.dot(unpack if last else pack, out, preferred_element_type=jnp.float32)
        both = both.astype(jnp.bfloat16).reshape(NZ, rows, size)
        if last:
            both = lax.all_to_all(both, "z", 0, 0, tiled=True)
            total = jnp.sum(both.astype(jnp.float32), axis=0)
        else:
            total = both[0].astype(jnp.float32)
            for place in STEPS:
                term = along_z(both[place], -place if place <= NZ // 2 else place - NZ // 2)
                total = total + term.astype(jnp.float32)
        mixed.append(total.astype(jnp.bfloat16))
    return jnp.concatenate(mixed, axis=1)


def solution(mesh):
    fine = Mesh(mesh.devices.reshape(NYL, NZ, NX, NYH, NC), AXES)
    rows = P(AXES, None)
    weights = P(("yl", "z", "x"), None, ("yh", "core"))
    return jax.shard_map(
        local,
        mesh=fine,
        in_specs=(rows, rows, rows, weights, weights, weights),
        out_specs=rows,
        check_vma=False,
    )
```

```python
import jax
import jax.numpy as jnp
from jax import lax
from jax.experimental.layout import Layout, with_layout_constraint
from jax.sharding import Mesh, PartitionSpec as P

NYL, NZ, NX, NYH, NC = 2, 8, 4, 2, 2
AXES = ("yl", "z", "x", "yh", "core")
CAP = 9
EXTRA = 128
OUT = (1792, 2304)
UP = 1024
LOOPED = (True, True)


def plane_groups():
    def index(yl, z, x, yh, core):
        return (((yl * NZ + z) * NX + x) * NYH + yh) * NC + core

    groups = []
    for z in range(NZ):
        for core in range(NC):
            for half in range(NYH):
                groups.append(
                    [index(yl, z, x, half ^ (yl if core else 0), core) for yl in range(NYL) for x in range(NX)]
                )
    return groups


def exchange(block):
    return lax.all_to_all(
        block, AXES, 0, 0, axis_index_groups=plane_groups(), tiled=True
    )


def swap(block, axis):
    return lax.ppermute(block, axis, [(0, 1), (1, 0)])


def along_z(block, step):
    return lax.ppermute(block, "z", [(i, (i + step) % NZ) for i in range(NZ)])


def parts_of(value, count):
    parts = []
    for _ in range(count):
        part = value.astype(jnp.bfloat16)
        value = value - part.astype(jnp.float32)
        parts.append(part)
    return parts


def summed(blocks, looped):
    middle = NZ // 2

    def turn(hop, state):
        down, up = state
        down = along_z(down.astype(jnp.bfloat16), -1)
        up = along_z(up.astype(jnp.bfloat16), 1)
        down = down.astype(jnp.float32) + blocks[1 + hop].astype(jnp.float32)
        up = up.astype(jnp.float32) + blocks[NZ - 2 - hop].astype(jnp.float32)
        return down, up

    state = blocks[0].astype(jnp.float32), blocks[NZ - 1].astype(jnp.float32)
    if looped:
        state = lax.fori_loop(0, middle - 1, turn, state)
    else:
        for hop in range(middle - 1):
            state = turn(hop, state)
    down, up = state
    down = along_z(down.astype(jnp.bfloat16), -1)
    return (down.astype(jnp.float32) + up).astype(jnp.bfloat16)


def local(tokens, expert_ids, gate_values, gate_weight, up_weight, down_weight):
    rows, width = tokens.shape
    top = expert_ids.shape[1]
    dests = NYL * NX
    cap = CAP * NZ

    own_gate, own_up, own_down = gate_weight[0], up_weight[0], down_weight[0]
    near_gate, near_up, near_down = swap(own_gate, "core"), swap(own_up, "core"), swap(own_down, "core")

    def pieces(own, near, start, size):
        own = own[start : start + size]
        far = swap(own, "yh")
        hop = swap(far, "core")
        return jnp.concatenate([own, near[start : start + size], far, hop], axis=1)

    gate = pieces(own_gate, near_gate, 0, width)
    up0 = pieces(own_up, near_up, 0, UP)
    up1 = pieces(own_up, near_up, UP, width - UP)
    downs = [pieces(own_down, near_down, 0, OUT[0]), pieces(own_down, near_down, OUT[0], OUT[1])]

    notes = jnp.concatenate([expert_ids.astype(jnp.bfloat16)] + parts_of(gate_values, 2), axis=1)
    notes = jnp.pad(notes, ((0, 0), (0, EXTRA - notes.shape[1])))
    own = jnp.concatenate([notes, tokens], axis=1)
    whole = jnp.broadcast_to(own[None], (NZ,) + own.shape).reshape(NZ * rows, own.shape[1])

    def turn(hop, state):
        whole, ahead, behind = state
        ahead = along_z(ahead, 1)
        behind = along_z(behind, -1)
        whole = lax.dynamic_update_slice(whole, ahead, ((NZ // 2 - 1 - hop) * rows, 0))
        whole = lax.dynamic_update_slice(whole, behind, ((NZ // 2 + 1 + hop) * rows, 0))
        return whole, ahead, behind

    whole, ahead, _ = lax.fori_loop(0, NZ // 2 - 1, turn, (whole, own, own))
    ahead = along_z(ahead, 1)
    whole = lax.dynamic_update_slice(whole, ahead, (0, 0))
    whole = with_layout_constraint(whole, Layout(major_to_minor=(0, 1)))

    count = NZ * rows
    notes = whole[:, : 3 * top].astype(jnp.float32)
    ids = notes[:, :top].astype(jnp.int32)
    values = notes[:, top : 2 * top] + notes[:, 2 * top :]
    dest = jnp.arange(dests, dtype=jnp.int32)
    expert = (dest // NX) * (NZ * NX) + lax.axis_index("z") * NX + dest % NX
    hit = ids[:, :, None] == expert[None, None, :]
    named = jnp.any(hit, axis=1)
    weight = jnp.sum(jnp.where(hit, values[:, :, None], 0.0), axis=1)
    order = jnp.arange(count, dtype=jnp.int32)
    before = (order[None, :] < order[:, None]).astype(jnp.bfloat16)
    rank = jnp.dot(before, named.astype(jnp.bfloat16), preferred_element_type=jnp.float32).astype(jnp.int32)
    slot = jnp.where(named, rank + cap * dest[None, :], -1)
    slots = jnp.arange(dests * cap, dtype=jnp.int32)

    def placed(slot):
        return (jnp.repeat(slot, cap, axis=1) == slots[None, :]).astype(jnp.bfloat16)

    pack = placed(slot)

    weights = jnp.pad(jnp.concatenate(parts_of(weight, 2), axis=1), ((0, 0), (0, EXTRA - 2 * dests)))
    whole = lax.dynamic_update_slice(whole, weights, (0, 0))
    packed = lax.dot_general(pack, whole, (((0,), (0,)), ((), ())), preferred_element_type=jnp.float32)
    packed = packed.astype(jnp.bfloat16).reshape(dests, cap, EXTRA + width)
    arrived = exchange(packed).reshape(dests * cap, EXTRA + width)
    mine = lax.axis_index("yl") * NX + lax.axis_index("x")
    weight = arrived[:, : 2 * dests].astype(jnp.float32)
    weight = jnp.where(jnp.arange(2 * dests) % dests == mine, weight, 0.0)
    weight = jnp.sum(weight, axis=1, keepdims=True)
    arrived = arrived[:, EXTRA:]

    gate_part = jnp.dot(arrived, gate, preferred_element_type=jnp.float32)
    up_part = jnp.dot(arrived[:, :UP], up0, preferred_element_type=jnp.float32)
    up_part = jnp.dot(arrived[:, UP:], up1, preferred_element_type=jnp.float32) + up_part
    hidden = (jax.nn.silu(gate_part) * up_part).astype(jnp.bfloat16)

    mixed = []
    for c, size in enumerate(OUT):
        out = lax.dot_general(hidden, downs[c], (((1,), (1,)), ((), ())), preferred_element_type=jnp.float32)
        out = (out * weight).astype(jnp.bfloat16).reshape(dests, cap, size)
        out = exchange(out).reshape(dests * cap, size)
        both = jnp.dot(pack, out, preferred_element_type=jnp.float32)
        both = both.astype(jnp.bfloat16).reshape(NZ, rows, size)
        mixed.append(summed(both, looped=LOOPED[c]))
    return jnp.concatenate(mixed, axis=1)


def solution(mesh):
    fine = Mesh(mesh.devices.reshape(NYL, NZ, NX, NYH, NC), AXES)
    rows = P(AXES, None)
    weights = P(("yl", "z", "x"), None, ("yh", "core"))
    return jax.shard_map(
        local,
        mesh=fine,
        in_specs=(rows, rows, rows, weights, weights, weights),
        out_specs=rows,
        check_vma=False,
    )
```

```python
import jax
import jax.numpy as jnp
from jax import lax
from jax.experimental.layout import Layout, with_layout_constraint
from jax.sharding import Mesh, PartitionSpec as P

NYL, NZ, NX, NYH, NC = 2, 8, 4, 2, 2
AXES = ("yl", "z", "x", "yh", "core")
CAP = 9
EXTRA = 128
OUT = (2304, 1792)
UP = 2048
LOOPED = (True, True)


def plane_groups():
    def index(yl, z, x, yh, core):
        return (((yl * NZ + z) * NX + x) * NYH + yh) * NC + core

    groups = []
    for z in range(NZ):
        for core in range(NC):
            for half in range(NYH):
                groups.append(
                    [index(yl, z, x, half ^ (yl if core else 0), core) for yl in range(NYL) for x in range(NX)]
                )
    return groups


def exchange(block):
    return lax.all_to_all(
        block, AXES, 0, 0, axis_index_groups=plane_groups(), tiled=True
    )


def swap(block, axis):
    return lax.ppermute(block, axis, [(0, 1), (1, 0)])


def along_z(block, step):
    return lax.ppermute(block, "z", [(i, (i + step) % NZ) for i in range(NZ)])


def parts_of(value, count):
    parts = []
    for _ in range(count):
        part = value.astype(jnp.bfloat16)
        value = value - part.astype(jnp.float32)
        parts.append(part)
    return parts


def summed(blocks, looped):
    middle = NZ // 2

    def turn(hop, state):
        down, up = state
        down = along_z(down.astype(jnp.bfloat16), -1)
        up = along_z(up.astype(jnp.bfloat16), 1)
        down = down.astype(jnp.float32) + blocks[1 + hop].astype(jnp.float32)
        up = up.astype(jnp.float32) + blocks[NZ - 2 - hop].astype(jnp.float32)
        return down, up

    state = blocks[0].astype(jnp.float32), blocks[NZ - 1].astype(jnp.float32)
    if looped:
        state = lax.fori_loop(0, middle - 1, turn, state)
    else:
        for hop in range(middle - 1):
            state = turn(hop, state)
    down, up = state
    down = along_z(down.astype(jnp.bfloat16), -1)
    return (down.astype(jnp.float32) + up).astype(jnp.bfloat16)


def local(tokens, expert_ids, gate_values, gate_weight, up_weight, down_weight):
    rows, width = tokens.shape
    top = expert_ids.shape[1]
    dests = NYL * NX
    cap = CAP * NZ

    own_gate, own_up, own_down = gate_weight[0], up_weight[0], down_weight[0]

    def pieces(own, start, size):
        own = own[start : start + size]
        far = swap(own, "yh")
        near = swap(own, "core")
        hop = swap(far, "core")
        return jnp.concatenate([own, near, far, hop], axis=1)

    gate = pieces(own_gate, 0, width)
    up0 = pieces(own_up, 0, UP)
    up1 = pieces(own_up, UP, width - UP)
    downs = [pieces(own_down, 0, OUT[0]), pieces(own_down, OUT[0], OUT[1])]

    notes = jnp.concatenate([expert_ids.astype(jnp.bfloat16)] + parts_of(gate_values, 2), axis=1)
    notes = jnp.pad(notes, ((0, 0), (0, EXTRA - notes.shape[1])))
    own = jnp.concatenate([notes, tokens], axis=1)
    whole = jnp.broadcast_to(own[None], (NZ,) + own.shape).reshape(NZ * rows, own.shape[1])

    def turn(hop, state):
        whole, ahead, behind = state
        ahead = along_z(ahead, 1)
        behind = along_z(behind, -1)
        whole = lax.dynamic_update_slice(whole, ahead, ((NZ // 2 - 1 - hop) * rows, 0))
        whole = lax.dynamic_update_slice(whole, behind, ((NZ // 2 + 1 + hop) * rows, 0))
        return whole, ahead, behind

    whole, ahead, _ = lax.fori_loop(0, NZ // 2 - 1, turn, (whole, own, own))
    ahead = along_z(ahead, 1)
    whole = lax.dynamic_update_slice(whole, ahead, (0, 0))
    whole = with_layout_constraint(whole, Layout(major_to_minor=(0, 1)))

    count = NZ * rows
    notes = whole[:, : 3 * top].astype(jnp.float32)
    ids = notes[:, :top].astype(jnp.int32)
    values = notes[:, top : 2 * top] + notes[:, 2 * top :]
    dest = jnp.arange(dests, dtype=jnp.int32)
    expert = (dest // NX) * (NZ * NX) + lax.axis_index("z") * NX + dest % NX
    hit = ids[:, :, None] == expert[None, None, :]
    named = jnp.any(hit, axis=1)
    weight = jnp.sum(jnp.where(hit, values[:, :, None], 0.0), axis=1)
    order = jnp.arange(count, dtype=jnp.int32)
    before = (order[None, :] < order[:, None]).astype(jnp.bfloat16)
    rank = jnp.dot(before, named.astype(jnp.bfloat16), preferred_element_type=jnp.float32).astype(jnp.int32)
    slot = jnp.where(named, rank + cap * dest[None, :], -1)
    slots = jnp.arange(dests * cap, dtype=jnp.int32)

    def placed(slot):
        return (jnp.repeat(slot, cap, axis=1) == slots[None, :]).astype(jnp.bfloat16)

    pack = placed(slot)

    weights = jnp.pad(jnp.concatenate(parts_of(weight, 2), axis=1), ((0, 0), (0, EXTRA - 2 * dests)))
    whole = lax.dynamic_update_slice(whole, weights, (0, 0))
    packed = lax.dot_general(pack, whole, (((0,), (0,)), ((), ())), preferred_element_type=jnp.float32)
    packed = packed.astype(jnp.bfloat16).reshape(dests, cap, EXTRA + width)
    arrived = exchange(packed).reshape(dests * cap, EXTRA + width)
    mine = lax.axis_index("yl") * NX + lax.axis_index("x")
    weight = arrived[:, : 2 * dests].astype(jnp.float32)
    weight = jnp.where(jnp.arange(2 * dests) % dests == mine, weight, 0.0)
    weight = jnp.sum(weight, axis=1, keepdims=True)
    arrived = arrived[:, EXTRA:]

    gate_part = jnp.dot(arrived, gate, preferred_element_type=jnp.float32)
    up_part = jnp.dot(arrived[:, :UP], up0, preferred_element_type=jnp.float32)
    up_part = jnp.dot(arrived[:, UP:], up1, preferred_element_type=jnp.float32) + up_part
    hidden = (jax.nn.silu(gate_part) * up_part).astype(jnp.bfloat16)

    mixed = []
    for c, size in enumerate(OUT):
        out = lax.dot_general(hidden, downs[c], (((1,), (1,)), ((), ())), preferred_element_type=jnp.float32)
        out = (out * weight).astype(jnp.bfloat16).reshape(dests, cap, size)
        out = exchange(out).reshape(dests * cap, size)
        both = jnp.dot(pack, out, preferred_element_type=jnp.float32)
        both = both.astype(jnp.bfloat16).reshape(NZ, rows, size)
        mixed.append(summed(both, looped=LOOPED[c]))
    return jnp.concatenate(mixed, axis=1)


def solution(mesh):
    fine = Mesh(mesh.devices.reshape(NYL, NZ, NX, NYH, NC), AXES)
    rows = P(AXES, None)
    weights = P(("yl", "z", "x"), None, ("yh", "core"))
    return jax.shard_map(
        local,
        mesh=fine,
        in_specs=(rows, rows, rows, weights, weights, weights),
        out_specs=rows,
        check_vma=False,
    )
```

```python
import jax
import jax.numpy as jnp
from jax import lax
from jax.experimental.layout import Layout, with_layout_constraint
from jax.sharding import Mesh, PartitionSpec as P

NYL, NZ, NX, NYH, NC = 2, 8, 4, 2, 2
AXES = ("yl", "z", "x", "yh", "core")
CAP = 9
EXTRA = 128
OUT = (1920, 2176)
HALF = 2048


def plane_groups():
    def index(yl, z, x, yh, core):
        return (((yl * NZ + z) * NX + x) * NYH + yh) * NC + core

    groups = []
    for z in range(NZ):
        for core in range(NC):
            for half in range(NYH):
                groups.append(
                    [index(yl, z, x, half ^ (yl if core else 0), core) for yl in range(NYL) for x in range(NX)]
                )
    return groups


def exchange(block):
    return lax.all_to_all(
        block, AXES, 0, 0, axis_index_groups=plane_groups(), tiled=True
    )


def swap(block, axis):
    return lax.ppermute(block, axis, [(0, 1), (1, 0)])


def along_z(block, step):
    return lax.ppermute(block, "z", [(i, (i + step) % NZ) for i in range(NZ)])


def parts_of(value, count):
    parts = []
    for _ in range(count):
        part = value.astype(jnp.bfloat16)
        value = value - part.astype(jnp.float32)
        parts.append(part)
    return parts


def around(own):
    rows, middle = own.shape[0], NZ // 2
    whole = jnp.broadcast_to(own[None], (NZ,) + own.shape).reshape(NZ * rows, own.shape[1])

    def turn(hop, state):
        whole, ahead, behind = state
        ahead = along_z(ahead, 1)
        behind = along_z(behind, -1)
        whole = lax.dynamic_update_slice(whole, behind, (lax.rem(middle + 1 + hop, NZ) * rows, 0))
        whole = lax.dynamic_update_slice(whole, ahead, ((middle - 1 - hop) * rows, 0))
        return whole, ahead, behind

    whole = lax.fori_loop(0, middle, turn, (whole, own, own))[0]
    return with_layout_constraint(whole, Layout(major_to_minor=(0, 1)))


def summed(blocks):
    middle = NZ // 2

    def turn(hop, state):
        down, up = state
        down = along_z(down.astype(jnp.bfloat16), -1).astype(jnp.float32)
        up = along_z(up.astype(jnp.bfloat16), 1).astype(jnp.float32)
        down = down + blocks[1 + hop].astype(jnp.float32)
        up = up + jnp.where(hop < middle - 1, blocks[NZ - 1 - hop].astype(jnp.float32), 0.0)
        return down, up

    first = blocks[0].astype(jnp.float32)
    down, up = lax.fori_loop(0, middle, turn, (first, jnp.zeros_like(first)))
    return (down + up).astype(jnp.bfloat16)


def local(tokens, expert_ids, gate_values, gate_weight, up_weight, down_weight):
    rows, width = tokens.shape
    top = expert_ids.shape[1]
    dests = NYL * NX
    cap = CAP * NZ

    own_gate, own_up, own_down = gate_weight[0], up_weight[0], down_weight[0]

    def pieces(own, start, size):
        own = own[start : start + size]
        far = swap(own, "yh")
        near = swap(own, "core")
        hop = swap(far, "core")
        return jnp.concatenate([own, near, far, hop], axis=1)

    gate = pieces(own_gate, 0, width)
    up0 = pieces(own_up, 0, HALF)
    up1 = pieces(own_up, HALF, width - HALF)
    downs = [pieces(own_down, 0, OUT[0]), pieces(own_down, OUT[0], OUT[1])]

    notes = jnp.concatenate([expert_ids.astype(jnp.bfloat16)] + parts_of(gate_values, 2), axis=1)
    notes = jnp.pad(notes, ((0, 0), (0, EXTRA - notes.shape[1])))
    whole = around(jnp.concatenate([notes, tokens[:, :HALF]], axis=1))
    rest = around(tokens[:, HALF:])

    count = NZ * rows
    notes = whole[:, : 3 * top].astype(jnp.float32)
    ids = notes[:, :top].astype(jnp.int32)
    values = notes[:, top : 2 * top] + notes[:, 2 * top :]
    dest = jnp.arange(dests, dtype=jnp.int32)
    expert = (dest // NX) * (NZ * NX) + lax.axis_index("z") * NX + dest % NX
    hit = ids[:, :, None] == expert[None, None, :]
    named = jnp.any(hit, axis=1)
    weight = jnp.sum(jnp.where(hit, values[:, :, None], 0.0), axis=1)
    order = jnp.arange(count, dtype=jnp.int32)
    before = (order[None, :] < order[:, None]).astype(jnp.bfloat16)
    rank = jnp.dot(before, named.astype(jnp.bfloat16), preferred_element_type=jnp.float32).astype(jnp.int32)
    slot = jnp.where(named, rank + cap * dest[None, :], -1)
    slots = jnp.arange(dests * cap, dtype=jnp.int32)

    def placed(slot):
        return (jnp.repeat(slot, cap, axis=1) == slots[None, :]).astype(jnp.bfloat16)

    pack = placed(slot)

    weights = jnp.pad(jnp.concatenate(parts_of(weight, 2), axis=1), ((0, 0), (0, EXTRA - 2 * dests)))
    whole = lax.dynamic_update_slice(whole, weights, (0, 0))

    def sent(block):
        packed = lax.dot_general(pack, block, (((0,), (0,)), ((), ())), preferred_element_type=jnp.float32)
        packed = packed.astype(jnp.bfloat16).reshape(dests, cap, block.shape[1])
        return exchange(packed).reshape(dests * cap, block.shape[1])

    arrived = sent(whole)
    others = sent(rest)
    mine = lax.axis_index("yl") * NX + lax.axis_index("x")
    weight = arrived[:, : 2 * dests].astype(jnp.float32)
    weight = jnp.where(jnp.arange(2 * dests) % dests == mine, weight, 0.0)
    weight = jnp.sum(weight, axis=1, keepdims=True)
    arrived = arrived[:, EXTRA:]

    gate_part = jnp.dot(arrived, gate[:HALF], preferred_element_type=jnp.float32)
    up_part = jnp.dot(arrived, up0, preferred_element_type=jnp.float32)
    gate_part = jnp.dot(others, gate[HALF:], preferred_element_type=jnp.float32) + gate_part
    up_part = jnp.dot(others, up1, preferred_element_type=jnp.float32) + up_part
    hidden = (jax.nn.silu(gate_part) * up_part).astype(jnp.bfloat16)

    mixed = []
    for c, size in enumerate(OUT):
        out = lax.dot_general(hidden, downs[c], (((1,), (1,)), ((), ())), preferred_element_type=jnp.float32)
        out = (out * weight).astype(jnp.bfloat16).reshape(dests, cap, size)
        out = exchange(out).reshape(dests * cap, size)
        both = jnp.dot(pack, out, preferred_element_type=jnp.float32)
        both = both.astype(jnp.bfloat16).reshape(NZ, rows, size)
        mixed.append(summed(both))
    return jnp.concatenate(mixed, axis=1)


def solution(mesh):
    fine = Mesh(mesh.devices.reshape(NYL, NZ, NX, NYH, NC), AXES)
    rows = P(AXES, None)
    weights = P(("yl", "z", "x"), None, ("yh", "core"))
    return jax.shard_map(
        local,
        mesh=fine,
        in_specs=(rows, rows, rows, weights, weights, weights),
        out_specs=rows,
        check_vma=False,
    )
```
